128 devices in a mesh: tm: 4 (over z_lo, core), freq: 32 (over y, z_hi, x).
Axes of the slice: x: 4, y: 4, z: 4 (z_hi: 2, z_lo: 2; z = z_hi * 2 + z_lo), core: 2. Of those that a mesh axis runs over, the one named last changes fastest.
Arguments:
- voltages: bfloat16 [4, 1024, 258048], P('tm', 'freq'), may hold values from -6 to 6
- chan_bins: int32 [128], replicated, may hold values from 0 to 2047, as said below
- antenna_map: int32 [1024], replicated, may hold values from 0 to 1023, each once
- beam_index: int32 [512], replicated, may hold values from 0 to 511, each once
- delays: float32 [512, 1024], replicated, may hold values from -4 to 4
Outputs:
- visibilities: float32 [128, 2, 1024, 1024], P(('tm', 'freq'))
- beam_volts: float32 [512, 128, 2, 192], P('freq', 'tm')
The draws below stay inside these ranges and needn't reach their ends.
Inputs may be any that keep to these rules, and one draw needn't show every extreme that they name: `chan_bins`: the 128 bins are distinct, below 2048. `antenna_map`: each signal feeds exactly one antenna input. `beam_index`: each beam has a pointing of its own.
All inputs are finite; a program needn't handle non-finite values.
Results may differ from the reference program's by a relative error of at most 0.006.
Values may be sent and summed in bfloat16 or wider, within the bound.
A program may use at most 128 MiB of HBM per device.

```python
import math
import jax
import jax.numpy as jnp
from jax import lax

SIG = 1024
NFFT = 4096
TAPS = 16
FR = 48
BEAMS = 512
POINTINGS = 512
TBLOCKS = 4
TIME = 192
CHANNELS = 128


def draw_chan_bins(key, part):
    first_key, second_key = jax.random.split(key)
    half_bins = NFFT // 2
    middle = jax.random.permutation(first_key, half_bins - 2)[:CHANNELS - 2] + 1
    values = jnp.concatenate([jnp.array([0, half_bins - 1], jnp.int32), middle.astype(jnp.int32)])
    ordering = jax.random.permutation(second_key, CHANNELS)
    return values[ordering]


def levels(rng, dims, cuts, smallest, high):
    gain, own = 1.0, jax.random.fold_in(rng, 6)
    for axis_at, blocks in cuts:
        draws = jnp.exp(jax.random.uniform(jax.random.fold_in(own, axis_at), (blocks,), jnp.float32, smallest / len(cuts), high / len(cuts)))
        gain = gain * jnp.repeat(draws, dims[axis_at] // blocks).reshape([-1 if axis == axis_at else 1 for axis in range(len(dims))])
    return gain


def bell_draw(key, dims, scale, limit, shards=(), kind=jnp.bfloat16):
    values = scale * jax.random.normal(key, dims, jnp.float32)
    if shards:
        values = values * levels(key, dims, shards, -0.22, 0.18)
    return jnp.clip(values, -limit, limit).astype(kind)


def setup_inputs(seed: int = 0) -> dict:
    key_list = jax.random.split(jax.random.key(seed), 6)
    voltages = bell_draw(key_list[0], (TBLOCKS, SIG, (FR + TAPS - 1) * NFFT), 1.0, 6.0, ((0, 4), (1, 32)))
    chan_bins = draw_chan_bins(jax.random.fold_in(key_list[5], 71), 0)
    antenna_map = jax.random.permutation(key_list[2], SIG).astype(jnp.int32)
    beam_index = jax.random.permutation(key_list[3], BEAMS).astype(jnp.int32)
    delays = jnp.clip(jax.random.uniform(key_list[4], (POINTINGS, SIG), jnp.float32, -4.0, 4.0), -4.0, 4.0)
    return {"voltages": voltages, "chan_bins": chan_bins, "antenna_map": antenna_map, "beam_index": beam_index, "delays": delays}


def prototype(tap_count, length):
    total = tap_count * length
    offsets = jnp.arange(total, dtype=jnp.float32)
    shifted = (offsets - 0.5 * total + 0.5) / length
    window = 0.5 - 0.5 * jnp.cos(2.0 * math.pi / total * (offsets + 0.5))
    return (jnp.sinc(shifted) * window).reshape(tap_count, length)

def dft_table(bins, length):
    positions = jnp.arange(length, dtype=jnp.int32)
    products = bins[:, None].astype(jnp.int32) * positions[None, :] % length
    angles = products.astype(jnp.float32) * (2.0 * math.pi / length)
    scale = 1.0 / math.sqrt(length)
    return jnp.stack([jnp.cos(angles) * scale, -jnp.sin(angles) * scale]).astype(jnp.bfloat16)

def filter_bank(samples, taps_table, frames):
    total = jnp.zeros((samples.shape[0], frames, samples.shape[2]), jnp.float32)
    for tap_index in range(taps_table.shape[0]):
        total = total + taps_table[tap_index] * samples[:, tap_index:tap_index + frames, :].astype(jnp.float32)
    return total.astype(jnp.bfloat16)

def correlate(volts):
    wide = volts.astype(jnp.float32)
    swapped = jnp.stack([wide[1], -wide[0]])
    real_part = jnp.einsum('rat,rbt->ab', wide, wide)
    imag_part = jnp.einsum('rat,rbt->ab', swapped, wide)
    return jnp.stack([real_part, imag_part]) / volts.shape[2]

def form_beams(volts, selected, bin_value):
    phase = selected * bin_value.astype(jnp.float32) * (2.0 * math.pi / NFFT)
    cosine = jnp.cos(phase).astype(jnp.bfloat16)
    sine = jnp.sin(phase).astype(jnp.bfloat16)
    weights = jnp.stack([jnp.stack([cosine, sine], 1), jnp.stack([-sine, cosine], 1)])
    formed = jnp.einsum('obra,rat->bot', weights.astype(jnp.float32), volts.astype(jnp.float32))
    return formed * (1.0 / math.sqrt(SIG))

def reference(voltages, chan_bins, antenna_map, beam_index, delays):
    taps_table = prototype(TAPS, NFFT)
    table = dft_table(chan_bins, NFFT)
    group = min(SIG, 128)

    def one_group(samples):
        shaped = samples.reshape(group, FR + TAPS - 1, NFFT)
        filtered = filter_bank(shaped, taps_table, FR)
        spectra = jnp.einsum('rcn,gjn->crgj', table.astype(jnp.float32), filtered.astype(jnp.float32))
        return spectra.astype(jnp.bfloat16)

    def one_block(block):
        return lax.map(one_group, block.reshape(SIG // group, group, block.shape[1]))
    spectra = lax.map(one_block, voltages)
    series = spectra.transpose(2, 3, 1, 4, 0, 5).reshape(CHANNELS, 2, SIG, TIME)
    selected = jnp.take(delays, beam_index, axis=0)

    def one_channel(inputs):
        stacked, bin_value = inputs
        volts = jnp.take(stacked, antenna_map, axis=1)
        return (correlate(volts), form_beams(volts, selected, bin_value))
    visibilities, beams = lax.map(one_channel, (series, chan_bins))
    return (visibilities, beams.transpose(1, 0, 2, 3))
```

```python
import functools
import math

import jax
import jax.numpy as jnp
import numpy as np
from jax import lax
from jax.experimental import pallas as pl
from jax.experimental.pallas import tpu as pltpu
from jax.sharding import PartitionSpec as P

NFFT = 4096
TAPS = 16
JB = 16
CHUNKS = 3
TM = 4
FREQ = 32
NDEV = TM * FREQ
SIGD = 32
CHAN = 128
BEAMS = 512
ANT = 1024
CENTRAL = (7, 8)
MESH = pl.DeviceIdType.MESH
f32 = jnp.float32
bf16 = jnp.bfloat16
i32 = jnp.int32


def prototype():
    total = TAPS * NFFT
    offsets = np.arange(total, dtype=np.float64)
    shifted = (offsets - 0.5 * total + 0.5) / NFFT
    window = 0.5 - 0.5 * np.cos(2.0 * math.pi / total * (offsets + 0.5))
    return (np.sinc(shifted) * window).reshape(TAPS, NFFT).astype(np.float32)


def turns(u):
    whole = jnp.floor(u + 0.5)
    theta = (u - whole) * (0.5 * math.pi)
    sq = theta * theta
    sin = theta * (1.0 + sq * (-1.0 / 6 + sq * (1.0 / 120 + sq * (-1.0 / 5040 + sq * (1.0 / 362880)))))
    cos = 1.0 + sq * (-0.5 + sq * (1.0 / 24 + sq * (-1.0 / 720 + sq * (1.0 / 40320))))
    quad = whole.astype(i32)
    odd = (quad & 1) != 0
    cos_out = jnp.where(odd, sin, cos)
    sin_out = jnp.where(odd, cos, sin)
    cos_out = jnp.where(((quad + 1) & 2) != 0, -cos_out, cos_out)
    sin_out = jnp.where((quad & 2) != 0, -sin_out, sin_out)
    return cos_out, sin_out


def column(row):
    return jnp.broadcast_to(row, (128, 128)).T


def lane_iota(rows=128, cols=128):
    return lax.broadcasted_iota(i32, (rows, cols), 1)


def main_kernel(
    v_hbm, taps_ref, bins_row, bins_smem, map_row, beam_row, delays_hbm,
    series_ref, beams_ref,
    vbuf, taps_b, table, filtered, spread, stage, recv, delays, weights, select, beam_sel,
    half, turned, xt, stage2, recv2, lanes_map,
    v_sem, d_sem, send_sem, recv_sem, send2_sem, recv2_sem,
):
    me_tm, me_f = lax.axis_index("tm"), lax.axis_index("freq")
    me = me_tm * FREQ + me_f
    barrier = pltpu.get_barrier_semaphore()

    first = JB + TAPS - 1
    quarter = NFFT // 4

    @pl.loop(0, 4)
    def _(nq):
        @pl.loop(0, first)
        def _(f):
            at = pl.ds(pl.multiple_of(f * NFFT + nq * quarter, quarter), quarter)
            pltpu.make_async_copy(v_hbm.at[0, :, at], vbuf.at[:, at], v_sem.at[nq]).start()

    for more in range(CHUNKS - 1):
        at = pl.ds((first + more * JB) * NFFT, JB * NFFT)
        pltpu.make_async_copy(v_hbm.at[0, :, at], vbuf.at[:, at], v_sem.at[4 + more]).start()
    delay_copy = pltpu.make_async_copy(delays_hbm, delays, d_sem)
    delay_copy.start()

    @pl.loop(1, NDEV)
    def _(i):
        peer = lax.rem(me + i, NDEV)
        pl.semaphore_signal(barrier, inc=1, device_id=(peer // FREQ, lax.rem(peer, FREQ)), device_id_type=MESH)

    @pl.loop(0, NFFT // 256)
    def _(nb):
        at = pl.ds(pl.multiple_of(nb * 256, 256), 256)
        for k in range(TAPS):
            taps_b[k, :, at] = jnp.broadcast_to(taps_ref[k : k + 1, at], (8, 256)).astype(bf16)

    bins_col = column(bins_row[...].astype(f32)).astype(i32)
    low_cos, low_sin = turns(((bins_col * lane_iota()) & (NFFT - 1)).astype(f32) * (4.0 / NFFT))
    high_cos, high_sin = turns(((bins_col * lane_iota()) & 31).astype(f32) * (4.0 / 32))
    scale = 1.0 / math.sqrt(NFFT)
    low_cos, low_sin = low_cos * scale, low_sin * scale
    for h in range(NFFT // 128):
        hc = jnp.broadcast_to(high_cos[:, h : h + 1], (128, 128))
        hs = jnp.broadcast_to(high_sin[:, h : h + 1], (128, 128))
        table[0:CHAN, h * 128 : (h + 1) * 128] = (low_cos * hc - low_sin * hs).astype(bf16)
        table[CHAN : 2 * CHAN, h * 128 : (h + 1) * 128] = (-(low_sin * hc + low_cos * hs)).astype(bf16)

    def filter_block(jc, nb, rb):
        c0 = pl.multiple_of(nb * 256, 256)
        at = pl.ds(c0, 256)
        outer = {k: taps_b[k, :, at] for k in range(TAPS) if k not in CENTRAL}
        central = {k: jnp.broadcast_to(taps_ref[k : k + 1, at], (8, 256)) for k in CENTRAL}
        small = [None] * JB
        large = [None] * JB
        for i in range(JB + TAPS - 1):
            x = vbuf[rb * 8 : (rb + 1) * 8, pl.ds(pl.multiple_of((jc * JB + i) * NFFT + c0, 256), 256)]
            wide = None
            for j in range(max(0, i - TAPS + 1), min(JB - 1, i) + 1):
                k = i - j
                if k in CENTRAL:
                    wide = x.astype(f32) if wide is None else wide
                    term = central[k] * wide
                    large[j] = term if large[j] is None else large[j] + term
                else:
                    term = outer[k] * x
                    small[j] = term if small[j] is None else small[j] + term
            j = i - TAPS + 1
            if j >= 0:
                filtered[rb * 128 + j * 8 : rb * 128 + (j + 1) * 8, at] = (large[j] + small[j].astype(f32)).astype(bf16)

    @pl.loop(0, CHUNKS)
    def _(jc):
        @pl.when(jc > 0)
        def _():
            at = pl.ds(0, JB * NFFT)
            pltpu.make_async_copy(v_hbm.at[0, :, at], vbuf.at[:, at], v_sem.at[3 + jc]).wait()

        @pl.loop(0, NFFT // 256)
        def _(nb):
            @pl.when((jc == 0) & (lax.rem(nb, 4) == 0))
            def _():
                at = pl.ds(0, first * quarter)
                pltpu.make_async_copy(v_hbm.at[0, :, at], vbuf.at[:, at], v_sem.at[nb // 4]).wait()

            for rb in range(SIGD // 8):
                filter_block(jc, nb, rb)

        for nt in range(2):
            out = lax.dot_general(
                table[...], filtered[nt * 256 : (nt + 1) * 256, :], (((1,), (1,)), ((), ())), preferred_element_type=f32
            )
            for r in range(2):
                for part in range(2):
                    rb = nt * 2 + part
                    spread[pl.ds(rb * 2 + r, CHAN, stride=8), :] = out[r * CHAN : (r + 1) * CHAN, part * 128 : (part + 1) * 128]

        @pl.loop(0, CHAN // 16)
        def _(cb):
            for i in range(16):
                c = cb * 16 + i
                stage[jc, c] = spread[pl.ds(pl.multiple_of(c * 8, 8), 8), :].astype(bf16)

        @pl.when(jc == 0)
        def _():
            pl.semaphore_wait(barrier, NDEV - 1)

        pltpu.make_async_copy(stage.at[jc, me], recv.at[jc, me], recv_sem.at[jc]).start()

        @pl.loop(1, NDEV)
        def _(i):
            peer = lax.rem(me + i, NDEV)
            pltpu.make_async_remote_copy(
                src_ref=stage.at[jc, peer], dst_ref=recv.at[jc, me], send_sem=send_sem.at[jc], recv_sem=recv_sem.at[jc],
                device_id=(peer // FREQ, lax.rem(peer, FREQ)), device_id_type=MESH,
            ).start()

    delay_copy.wait()
    bin_value = bins_smem[me].astype(f32)

    @pl.loop(0, BEAMS // 32)
    def _(pb):
        row = pl.multiple_of(pb * 32, 32)
        for part in range(4):
            cos, sin = turns(delays[pl.ds(row, 32), part * 256 : (part + 1) * 256] * bin_value * (4.0 / NFFT))
            weights[pl.ds(row, 32), part * 256 : (part + 1) * 256] = cos.astype(bf16)
            weights[pl.ds(BEAMS + row, 32), part * 256 : (part + 1) * 256] = sin.astype(bf16)

    lanes = lane_iota()
    signal = (lanes // 4) * SIGD + lax.rem(lanes, 4) * 8
    for ab in range(ANT // 128):
        wanted = column(map_row[:, ab * 128 : (ab + 1) * 128].astype(f32)).astype(i32)
        for s8 in range(8):
            select[ab * 128 : (ab + 1) * 128, s8 * 128 : (s8 + 1) * 128] = jnp.where(wanted == signal + s8, 1.0, 0.0).astype(bf16)
    for bb in range(BEAMS // 128):
        wanted = column(beam_row[:, bb * 128 : (bb + 1) * 128].astype(f32)).astype(i32)
        for pb in range(BEAMS // 128):
            beam_sel[bb * 128 : (bb + 1) * 128, pb * 128 : (pb + 1) * 128] = jnp.where(wanted == lanes + pb * 128, 1.0, 0.0).astype(bf16)
    for jc in range(CHUNKS):
        rows = lax.broadcasted_iota(i32, (128, 384), 0)
        to = (rows // 64) * 192 + (lax.rem(rows, 64) // 16) * 48 + jc * JB + lax.rem(rows, 16)
        lanes_map[jc * 128 : (jc + 1) * 128, :] = jnp.where(to == lane_iota(128, 384), 1.0, 0.0).astype(bf16)

    @pl.loop(0, CHUNKS)
    def _(jc):
        pltpu.make_async_copy(stage.at[jc], recv.at[jc], recv_sem.at[jc]).wait()

        @pl.loop(0, TM)
        def _(q):
            for f in range(FREQ):
                half[f * 8 : (f + 1) * 8, :] = recv[jc, q * FREQ + f].astype(f32)
            for r in range(2):
                turned[...] = half[pl.ds(r, 128, stride=2), :].T
                row = pl.multiple_of((r * TM + q) * JB, JB)
                for s8 in range(8):
                    xt[pl.ds(row, JB), s8 * 128 : (s8 + 1) * 128] = turned[pl.ds(s8, JB, stride=8), :].astype(bf16)

        at = pl.ds(pl.multiple_of(jc * 128, 128), 128)

        @pl.loop(0, ANT // 256)
        def _(ab):
            rows = pl.ds(pl.multiple_of(ab * 256, 256), 256)
            series_ref[rows, at] = lax.dot_general(
                select[rows, :], xt[...], (((1,), (1,)), ((), ())), preferred_element_type=f32
            ).astype(bf16)

        series = series_ref[:, at]
        sign = jnp.where(lane_iota(BEAMS // 2, 128) < 64, 1.0, -1.0)
        formed = []
        for pb in range(2):
            cos_part = jnp.dot(weights[pb * 256 : (pb + 1) * 256, :], series, preferred_element_type=f32)
            sin_part = jnp.dot(weights[BEAMS + pb * 256 : BEAMS + (pb + 1) * 256, :], series, preferred_element_type=f32)
            formed.append(((cos_part + sign * pltpu.roll(sin_part, 64, 1)) * (1.0 / math.sqrt(ANT))).astype(bf16))
        picked = jnp.dot(beam_sel[...], jnp.concatenate(formed, 0), preferred_element_type=f32).astype(bf16)
        stage2[jc] = picked.reshape(FREQ, 16, 128)

        pltpu.make_async_copy(stage2.at[jc, me_f], recv2.at[jc, me_f], recv2_sem.at[jc]).start()

        @pl.loop(1, FREQ)
        def _(i):
            peer = lax.rem(me_f + i, FREQ)
            pltpu.make_async_remote_copy(
                src_ref=stage2.at[jc, peer], dst_ref=recv2.at[jc, me_f], send_sem=send2_sem.at[jc], recv_sem=recv2_sem.at[jc],
                device_id=(me_tm, peer), device_id_type=MESH,
            ).start()

    for jc in range(CHUNKS):
        pltpu.make_async_copy(stage2.at[jc], recv2.at[jc], recv2_sem.at[jc]).wait()

    @pl.loop(0, FREQ // 8)
    def _(cb):
        total = None
        for jc in range(CHUNKS):
            part = recv2[jc, pl.ds(cb * 8, 8)].reshape(128, 128)
            term = jnp.dot(part, lanes_map[jc * 128 : (jc + 1) * 128, :], preferred_element_type=f32)
            total = term if total is None else total + term
        beams_ref[pl.ds(cb * 128, 128), :] = total

    for jc in range(CHUNKS):
        sent = stage.at[jc, pl.ds(0, NDEV - 1)]
        pltpu.make_async_copy(sent, sent, send_sem.at[jc]).wait()
        sent = stage2.at[jc, pl.ds(0, FREQ - 1)]
        pltpu.make_async_copy(sent, sent, send2_sem.at[jc]).wait()


def vis_kernel(rows_ref, all_ref, out_ref):
    rows = rows_ref[...]
    every = all_ref[...]
    nt = (((1,), (1,)), ((), ()))
    scale = 1.0 / 192.0
    out_ref[0, 0] = lax.dot_general(rows, every, nt, preferred_element_type=f32) * scale
    parts = []
    for jc in range(CHUNKS):
        part = rows[:, jc * 128 : (jc + 1) * 128].astype(f32)
        sign = jnp.where(lane_iota(*part.shape) < 64, 1.0, -1.0)
        parts.append((pltpu.roll(part, 64, 1) * sign).astype(bf16))
    swapped = jnp.concatenate(parts, 1)
    out_ref[0, 1] = lax.dot_general(swapped, every, nt, preferred_element_type=f32) * scale


def body(voltages, chan_bins, antenna_map, beam_index, delays):
    vmem = pl.BlockSpec(memory_space=pltpu.VMEM)
    anywhere = pl.BlockSpec(memory_space=pl.ANY)
    dma = pltpu.SemaphoreType.DMA
    series, beams = pl.pallas_call(
        main_kernel,
        out_shape=(
            jax.ShapeDtypeStruct((ANT, 384), bf16),
            jax.ShapeDtypeStruct((FREQ * 16, 384), f32),
        ),
        in_specs=[anywhere, vmem, vmem, pl.BlockSpec(memory_space=pltpu.SMEM), vmem, vmem, anywhere],
        out_specs=(vmem, vmem),
        scratch_shapes=[
            pltpu.VMEM((SIGD, 63 * NFFT), bf16),
            pltpu.VMEM((TAPS, 8, NFFT), bf16),
            pltpu.VMEM((2 * CHAN, NFFT), bf16),
            pltpu.VMEM((SIGD * JB, NFFT), bf16),
            pltpu.VMEM((CHAN * 8, 128), f32),
            pltpu.VMEM((CHUNKS, NDEV, 8, 128), bf16),
            pltpu.VMEM((CHUNKS, NDEV, 8, 128), bf16),
            pltpu.VMEM((BEAMS, ANT), f32),
            pltpu.VMEM((2 * BEAMS, ANT), bf16),
            pltpu.VMEM((ANT, ANT), bf16),
            pltpu.VMEM((BEAMS, BEAMS), bf16),
            pltpu.VMEM((256, 128), f32),
            pltpu.VMEM((128, 128), f32),
            pltpu.VMEM((128, ANT), bf16),
            pltpu.VMEM((CHUNKS, FREQ, 16, 128), bf16),
            pltpu.VMEM((CHUNKS, FREQ, 16, 128), bf16),
            pltpu.VMEM((384, 384), bf16),
            dma((6,)),
            dma,
            dma((CHUNKS,)),
            dma((CHUNKS,)),
            dma((CHUNKS,)),
            dma((CHUNKS,)),
        ],
        compiler_params=pltpu.CompilerParams(
            collective_id=0, has_side_effects=True, vmem_limit_bytes=60 * 1024 * 1024
        ),
        name="channelize",
    )(
        voltages,
        jnp.asarray(prototype()),
        chan_bins.reshape(1, CHAN),
        chan_bins,
        antenna_map.reshape(1, ANT),
        beam_index.reshape(1, BEAMS),
        delays,
    )
    block = 128
    visibilities = pl.pallas_call(
        vis_kernel,
        grid=(ANT // block,),
        out_shape=jax.ShapeDtypeStruct((1, 2, ANT, ANT), f32),
        in_specs=[pl.BlockSpec((block, 384), lambda i: (i, 0)), pl.BlockSpec((ANT, 384), lambda i: (0, 0))],
        out_specs=pl.BlockSpec((1, 2, block, ANT), lambda i: (0, 0, i, 0)),
        name="correlate",
    )(series, series)
    beam_volts = beams.reshape(FREQ, 16, 2, 192).transpose(1, 0, 2, 3)
    return (visibilities, beam_volts)


def solution(mesh):
    return jax.shard_map(
        body,
        mesh=mesh,
        in_specs=(P("tm", "freq", None), P(), P(), P(), P()),
        out_specs=(P(("tm", "freq"), None, None, None), P("freq", "tm", None, None)),
        check_vma=False,
    )
```

```python
import functools
import math

import jax
import jax.numpy as jnp
import numpy as np
from jax import lax
from jax.experimental import pallas as pl
from jax.experimental.pallas import tpu as pltpu
from jax.sharding import PartitionSpec as P

NFFT = 4096
TAPS = 16
JB = 16
CHUNKS = 3
TM = 4
FREQ = 32
NDEV = TM * FREQ
SIGD = 32
CHAN = 128
BEAMS = 512
ANT = 1024
CENTRAL = (7, 8)
EACH = 7
VSTEPS = 4
VMEM_LIMIT = 60 * 1024 * 1024
MESH = pl.DeviceIdType.MESH
f32 = jnp.float32
bf16 = jnp.bfloat16
i32 = jnp.int32


def prototype():
    total = TAPS * NFFT
    offsets = np.arange(total, dtype=np.float64)
    shifted = (offsets - 0.5 * total + 0.5) / NFFT
    window = 0.5 - 0.5 * np.cos(2.0 * math.pi / total * (offsets + 0.5))
    return (np.sinc(shifted) * window).reshape(TAPS, NFFT).astype(np.float32)


def turns(u):
    whole = jnp.floor(u + 0.5)
    theta = (u - whole) * (0.5 * math.pi)
    sq = theta * theta
    sin = theta * (1.0 + sq * (-1.0 / 6 + sq * (1.0 / 120 + sq * (-1.0 / 5040 + sq * (1.0 / 362880)))))
    cos = 1.0 + sq * (-0.5 + sq * (1.0 / 24 + sq * (-1.0 / 720 + sq * (1.0 / 40320))))
    quad = whole.astype(i32)
    odd = (quad & 1) != 0
    cos_out = jnp.where(odd, sin, cos)
    sin_out = jnp.where(odd, cos, sin)
    cos_out = jnp.where(((quad + 1) & 2) != 0, -cos_out, cos_out)
    sin_out = jnp.where((quad & 2) != 0, -sin_out, sin_out)
    return cos_out, sin_out


def column(row):
    return jnp.broadcast_to(row, (128, 128)).T


def lane_iota(rows=128, cols=128):
    return lax.broadcasted_iota(i32, (rows, cols), 1)


def main_kernel(
    v_hbm, taps_hbm, bins_hbm, bins_smem, map_hbm, beam_hbm, delays_hbm,
    series_hbm, beams_hbm,
    vbuf, taps_ref, bins_row, map_row, beam_row, taps_b, table, filtered, spread, stage, recv, delays, weights, select, beam_sel,
    half, turned, xt, series, stage2,
    v_sem, small_sem, d_sem, send_sem, recv_sem, send2_sem, recv2_sem, out_sem,
):
    me_tm, me_f = lax.axis_index("tm"), lax.axis_index("freq")
    me = me_tm * FREQ + me_f
    barrier = pltpu.get_barrier_semaphore()

    def peer_id(i):
        peer = (me + i) & (NDEV - 1)
        return peer, (peer >> 5, peer & (FREQ - 1))

    def greet(i):
        pl.semaphore_signal(barrier, inc=1, device_id=peer_id(i)[1], device_id_type=MESH)

    def send(jc, i):
        peer, where = peer_id(i)
        pltpu.make_async_remote_copy(
            src_ref=stage.at[jc, peer], dst_ref=recv.at[jc, me], send_sem=send_sem.at[jc], recv_sem=recv_sem.at[jc],
            device_id=where, device_id_type=MESH,
        ).start()

    def ahead(act):
        @pl.loop(1, NDEV - 16 * EACH)
        def _(i):
            act(i)

    def beside(step, act):
        for u in range(EACH):
            act(NDEV - 16 * EACH + step * EACH + u)

    first = JB + TAPS - 1
    quarter = NFFT // 4

    def fetch_quarter(nq):
        @pl.loop(0, first)
        def _(f):
            at = pl.ds(pl.multiple_of(f * NFFT + nq * quarter, quarter), quarter)
            pltpu.make_async_copy(v_hbm.at[0, :, at], vbuf.at[:, at], v_sem.at[nq]).start()

    smalls = [
        pltpu.make_async_copy(src, dst, small_sem.at[n])
        for n, (src, dst) in enumerate(((taps_hbm, taps_ref), (bins_hbm, bins_row), (map_hbm, map_row), (beam_hbm, beam_row)))
    ]
    for small in smalls:
        small.start()
    fetch_quarter(0)
    smalls[0].wait()

    @pl.loop(0, NFFT // 256)
    def _(nb):
        at = pl.ds(pl.multiple_of(nb * 256, 256), 256)
        for k in range(TAPS):
            taps_b[k, :, at] = jnp.broadcast_to(taps_ref[k : k + 1, at], (8, 256)).astype(bf16)

    @pl.loop(1, 4)
    def _(nq):
        fetch_quarter(nq)

    for more in range(CHUNKS - 1):
        at = pl.ds((first + more * JB) * NFFT, JB * NFFT)
        pltpu.make_async_copy(v_hbm.at[0, :, at], vbuf.at[:, at], v_sem.at[4 + more]).start()
    delay_copy = pltpu.make_async_copy(delays_hbm, delays, d_sem)
    delay_copy.start()

    for small in smalls[1:]:
        small.wait()
    bins_col = column(bins_row[...].astype(f32)).astype(i32)
    low_cos, low_sin = turns(((bins_col * lane_iota()) & (NFFT - 1)).astype(f32) * (4.0 / NFFT))
    high_cos, high_sin = turns(((bins_col * lane_iota()) & 31).astype(f32) * (4.0 / 32))
    scale = 1.0 / math.sqrt(NFFT)
    low_cos, low_sin = low_cos * scale, low_sin * scale
    for h in range(NFFT // 128):
        hc = jnp.broadcast_to(high_cos[:, h : h + 1], (128, 128))
        hs = jnp.broadcast_to(high_sin[:, h : h + 1], (128, 128))
        table[0:CHAN, h * 128 : (h + 1) * 128] = (low_cos * hc - low_sin * hs).astype(bf16)
        table[CHAN : 2 * CHAN, h * 128 : (h + 1) * 128] = (-(low_sin * hc + low_cos * hs)).astype(bf16)

    def filter_block(jc, nb, rb):
        c0 = pl.multiple_of(nb * 256, 256)
        at = pl.ds(c0, 256)
        outer = {k: taps_b[k, :, at] for k in range(TAPS) if k not in CENTRAL}
        central = {k: jnp.broadcast_to(taps_ref[k : k + 1, at], (8, 256)) for k in CENTRAL}
        small = [None] * JB
        large = [None] * JB
        for i in range(JB + TAPS - 1):
            x = vbuf[rb * 8 : (rb + 1) * 8, pl.ds(pl.multiple_of((jc * JB + i) * NFFT + c0, 256), 256)]
            wide = None
            for j in range(max(0, i - TAPS + 1), min(JB - 1, i) + 1):
                k = i - j
                if k in CENTRAL:
                    wide = x.astype(f32) if wide is None else wide
                    term = central[k] * wide
                    large[j] = term if large[j] is None else large[j] + term
                else:
                    term = outer[k] * x
                    small[j] = term if small[j] is None else small[j] + term
            j = i - TAPS + 1
            if j >= 0:
                filtered[rb * 128 + j * 8 : rb * 128 + (j + 1) * 8, at] = (large[j] + small[j].astype(f32)).astype(bf16)

    def channelize(jc, act):
        if jc > 0:
            at = pl.ds(0, JB * NFFT)
            pltpu.make_async_copy(v_hbm.at[0, :, at], vbuf.at[:, at], v_sem.at[3 + jc]).wait()
        ahead(act)
        @pl.loop(0, NFFT // 256)
        def _(nb):
            if jc == 0:
                @pl.when(lax.rem(nb, 4) == 0)
                def _():
                    at = pl.ds(0, first * quarter)
                    pltpu.make_async_copy(v_hbm.at[0, :, at], vbuf.at[:, at], v_sem.at[nb // 4]).wait()

            beside(nb, act)
            for rb in range(SIGD // 8):
                filter_block(jc, nb, rb)

        for nt in range(2):
            out = lax.dot_general(
                table[...], filtered[nt * 256 : (nt + 1) * 256, :], (((1,), (1,)), ((), ())), preferred_element_type=f32
            )
            for r in range(2):
                for part in range(2):
                    rb = nt * 2 + part
                    spread[pl.ds(rb * 2 + r, CHAN, stride=8), :] = out[r * CHAN : (r + 1) * CHAN, part * 128 : (part + 1) * 128]

        @pl.loop(0, CHAN // 16)
        def _(cb):
            for i in range(16):
                c = cb * 16 + i
                stage[jc, c] = spread[pl.ds(pl.multiple_of(c * 8, 8), 8), :].astype(bf16)

        if jc == 0:
            pl.semaphore_wait(barrier, NDEV - 1)
        pltpu.make_async_copy(stage.at[jc, me], recv.at[jc, me], recv_sem.at[jc]).start()

    channelize(0, greet)
    channelize(1, functools.partial(send, 0))
    channelize(2, functools.partial(send, 1))

    delay_copy.wait()
    bin_value = bins_smem[me].astype(f32) * (4.0 / NFFT)

    ahead(functools.partial(send, 2))

    @pl.loop(0, BEAMS // 32)
    def _(pb):
        beside(pb, functools.partial(send, 2))
        row = pl.multiple_of(pb * 32, 32)
        for part in range(4):
            cos, sin = turns(delays[pl.ds(row, 32), part * 256 : (part + 1) * 256] * bin_value)
            weights[pl.ds(row, 32), part * 256 : (part + 1) * 256] = cos.astype(bf16)
            weights[pl.ds(BEAMS + row, 32), part * 256 : (part + 1) * 256] = sin.astype(bf16)

    lanes = lane_iota()
    signal = (lanes // 4) * SIGD + lax.rem(lanes, 4) * 8
    for ab in range(ANT // 128):
        wanted = column(map_row[:, ab * 128 : (ab + 1) * 128].astype(f32)).astype(i32)
        for s8 in range(8):
            select[ab * 128 : (ab + 1) * 128, s8 * 128 : (s8 + 1) * 128] = jnp.where(wanted == signal + s8, 1.0, 0.0).astype(bf16)
    for bb in range(BEAMS // 128):
        wanted = column(beam_row[:, bb * 128 : (bb + 1) * 128].astype(f32)).astype(i32)
        for pb in range(BEAMS // 128):
            beam_sel[bb * 128 : (bb + 1) * 128, pb * 128 : (pb + 1) * 128] = jnp.where(wanted == lanes + pb * 128, 1.0, 0.0).astype(bf16)
    def beamform(low, high):
        for jc in range(low, high):
            pltpu.make_async_copy(stage.at[jc], recv.at[jc], recv_sem.at[jc]).wait()

            @pl.loop(0, TM)
            def _(q):
                for f in range(FREQ):
                    half[f * 8 : (f + 1) * 8, :] = recv[jc, q * FREQ + f].astype(f32)
                for r in range(2):
                    turned[...] = half[pl.ds(r, 128, stride=2), :].T
                    row = pl.multiple_of((jc - low) * 128 + (r * TM + q) * JB, JB)
                    for s8 in range(8):
                        xt[pl.ds(row, JB), s8 * 128 : (s8 + 1) * 128] = turned[pl.ds(s8, JB, stride=8), :].astype(bf16)

        count = high - low
        cols = slice(low * 128, high * 128)

        @pl.loop(0, ANT // 256)
        def _(ab):
            rows = pl.ds(pl.multiple_of(ab * 256, 256), 256)
            series[rows, cols] = lax.dot_general(
                select[rows, :], xt[0 : count * 128, :], (((1,), (1,)), ((), ())), preferred_element_type=f32
            ).astype(bf16)

        pltpu.make_async_copy(series.at[:, cols], series_hbm.at[:, cols], out_sem.at[low]).start()
        ordered = series[:, cols]
        sign = jnp.where(lane_iota(BEAMS // 2, 128) < 64, 1.0 / math.sqrt(ANT), -1.0 / math.sqrt(ANT))
        formed = []
        for pb in range(2):
            cos_part = jnp.dot(weights[pb * 256 : (pb + 1) * 256, :], ordered, preferred_element_type=f32)
            sin_part = jnp.dot(weights[BEAMS + pb * 256 : BEAMS + (pb + 1) * 256, :], ordered, preferred_element_type=f32)
            turn = [sign * pltpu.roll(sin_part[:, n * 128 : (n + 1) * 128], 64, 1) for n in range(count)]
            formed.append((cos_part * (1.0 / math.sqrt(ANT)) + jnp.concatenate(turn, 1)).astype(bf16))
        picked = jnp.dot(beam_sel[...], jnp.concatenate(formed, 0), preferred_element_type=f32)
        for jc in range(low, high):
            part = picked[:, (jc - low) * 128 : (jc - low + 1) * 128]
            stage2[jc] = part.astype(bf16).reshape(FREQ, 16, 128)
            pltpu.make_async_copy(stage2.at[jc, me_f], beams_hbm.at[jc, me_f], recv2_sem.at[jc]).start()

            @pl.loop(1, FREQ)
            def _(i):
                peer = (me_f + i) & (FREQ - 1)
                pltpu.make_async_remote_copy(
                    src_ref=stage2.at[jc, peer], dst_ref=beams_hbm.at[jc, me_f], send_sem=send2_sem.at[jc],
                    recv_sem=recv2_sem.at[jc], device_id=(me_tm, peer), device_id_type=MESH,
                ).start()

    beamform(0, 2)
    beamform(2, 3)

    for jc in range(CHUNKS):
        sent = stage.at[jc, pl.ds(0, NDEV - 1)]
        pltpu.make_async_copy(sent, sent, send_sem.at[jc]).wait()
        sent = stage2.at[jc, pl.ds(0, FREQ - 1)]
        pltpu.make_async_copy(sent, sent, send2_sem.at[jc]).wait()
    for low, high in ((0, 2), (2, 3)):
        cols = slice(low * 128, high * 128)
        pltpu.make_async_copy(series.at[:, cols], series_hbm.at[:, cols], out_sem.at[low]).wait()
    for jc in range(CHUNKS):
        pltpu.make_async_copy(stage2.at[jc], beams_hbm.at[jc], recv2_sem.at[jc]).wait()


def vis_kernel(series_ref, part_ref, beams_ref, vis_ref, out_ref):
    part = part_ref[...]
    swapped = []
    for jc in range(CHUNKS):
        chunk = part[:, jc * 128 : (jc + 1) * 128].astype(f32)
        sign = jnp.where(lane_iota(*chunk.shape) < 64, 1.0, -1.0)
        swapped.append((pltpu.roll(chunk, 64, 1) * sign).astype(bf16))
    pair = jnp.concatenate([part, jnp.concatenate(swapped, 1)], 0)
    count = ANT // VSTEPS
    for bb in range(4):
        cols = slice(bb * 256, (bb + 1) * 256)
        out = lax.dot_general(pair, series_ref[cols, :], (((1,), (1,)), ((), ())), preferred_element_type=f32)
        out = out * (1.0 / 192.0)
        vis_ref[0, 0, :, cols] = out[:count]
        vis_ref[0, 1, :, cols] = out[count:]

    @pl.when(pl.program_id(0) == VSTEPS // 2)
    def _():
        moves = []
        for jc in range(CHUNKS):
            rows = lax.broadcasted_iota(i32, (128, 512), 0)
            to = (rows >> 6) * 256 + ((rows >> 4) & 3) * 48 + jc * JB + (rows & 15)
            moves.append(jnp.where(to == lane_iota(128, 512), 1.0, 0.0).astype(bf16))
        moves = jnp.concatenate(moves, 0)
        for cb in range(4):
            found = jnp.concatenate([beams_ref[jc, cb * 128 : (cb + 1) * 128, :] for jc in range(CHUNKS)], 1)
            total = jnp.dot(found, moves, preferred_element_type=f32)
            for u in range(8):
                for r in range(2):
                    rows = slice(u * 16, (u + 1) * 16)
                    out_ref[:, cb * 8 + u, r, 0:128] = total[rows, r * 256 : r * 256 + 128]
                    out_ref[:, cb * 8 + u, r, 128:192] = total[rows, r * 256 + 128 : r * 256 + 192]


def body(voltages, chan_bins, antenna_map, beam_index, delays):
    hbm = pl.BlockSpec(memory_space=pltpu.HBM)
    anywhere = pl.BlockSpec(memory_space=pl.ANY)
    dma = pltpu.SemaphoreType.DMA
    series, beams = pl.pallas_call(
        main_kernel,
        out_shape=(
            jax.ShapeDtypeStruct((ANT, 384), bf16),
            jax.ShapeDtypeStruct((CHUNKS, FREQ, 16, 128), bf16),
        ),
        in_specs=[hbm, hbm, hbm, pl.BlockSpec(memory_space=pltpu.SMEM), hbm, hbm, hbm],
        out_specs=(anywhere, anywhere),
        scratch_shapes=[
            pltpu.VMEM((SIGD, 63 * NFFT), bf16),
            pltpu.VMEM((TAPS, NFFT), f32),
            pltpu.VMEM((1, CHAN), i32),
            pltpu.VMEM((1, ANT), i32),
            pltpu.VMEM((1, BEAMS), i32),
            pltpu.VMEM((TAPS, 8, NFFT), bf16),
            pltpu.VMEM((2 * CHAN, NFFT), bf16),
            pltpu.VMEM((SIGD * JB, NFFT), bf16),
            pltpu.VMEM((CHAN * 8, 128), f32),
            pltpu.VMEM((CHUNKS, NDEV, 8, 128), bf16),
            pltpu.VMEM((CHUNKS, NDEV, 8, 128), bf16),
            pltpu.VMEM((BEAMS, ANT), f32),
            pltpu.VMEM((2 * BEAMS, ANT), bf16),
            pltpu.VMEM((ANT, ANT), bf16),
            pltpu.VMEM((BEAMS, BEAMS), bf16),
            pltpu.VMEM((256, 128), f32),
            pltpu.VMEM((128, 128), f32),
            pltpu.VMEM((256, ANT), bf16),
            pltpu.VMEM((ANT, 384), bf16),
            pltpu.VMEM((CHUNKS, FREQ, 16, 128), bf16),
            dma((6,)),
            dma((4,)),
            dma,
            dma((CHUNKS,)),
            dma((CHUNKS,)),
            dma((CHUNKS,)),
            dma((CHUNKS,)),
            dma((CHUNKS,)),
        ],
        compiler_params=pltpu.CompilerParams(
            collective_id=0, has_side_effects=True, vmem_limit_bytes=VMEM_LIMIT
        ),
        name="channelize",
    )(
        voltages,
        jnp.asarray(prototype()),
        chan_bins.reshape(1, CHAN),
        chan_bins,
        antenna_map.reshape(1, ANT),
        beam_index.reshape(1, BEAMS),
        delays,
    )
    rows = ANT // VSTEPS
    visibilities, beam_volts = pl.pallas_call(
        vis_kernel,
        grid=(VSTEPS,),
        out_shape=(
            jax.ShapeDtypeStruct((1, 2, ANT, ANT), f32),
            jax.ShapeDtypeStruct((16, FREQ, 2, 192), f32),
        ),
        in_specs=[
            pl.BlockSpec(memory_space=pltpu.VMEM),
            pl.BlockSpec((rows, 384), lambda i: (i, 0)),
            pl.BlockSpec(memory_space=pltpu.VMEM),
        ],
        out_specs=(
            pl.BlockSpec((1, 2, rows, ANT), lambda i: (0, 0, i, 0)),
            pl.BlockSpec((16, FREQ, 2, 192), lambda i: (0, 0, 0, 0)),
        ),
        compiler_params=pltpu.CompilerParams(vmem_limit_bytes=VMEM_LIMIT),
        name="correlate",
    )(series, series, beams.reshape(CHUNKS, FREQ * 16, 128))
    return (visibilities, beam_volts)


def solution(mesh):
    return jax.shard_map(
        body,
        mesh=mesh,
        in_specs=(P("tm", "freq", None), P(), P(), P(), P()),
        out_specs=(P(("tm", "freq"), None, None, None), P("freq", "tm", None, None)),
        check_vma=False,
    )
```

```python
import functools
import math

import jax
import jax.numpy as jnp
import numpy as np
from jax import lax
from jax.experimental import pallas as pl
from jax.experimental.pallas import tpu as pltpu
from jax.sharding import PartitionSpec as P

NFFT = 4096
TAPS = 16
JB = 16
CHUNKS = 3
TM = 4
FREQ = 32
NDEV = TM * FREQ
SIGD = 32
CHAN = 128
BEAMS = 512
ANT = 1024
CENTRAL = (7, 8)
EACH = 7
VSTEPS = 4
VMEM_LIMIT = 60 * 1024 * 1024
MESH = pl.DeviceIdType.MESH
f32 = jnp.float32
bf16 = jnp.bfloat16
i32 = jnp.int32


def prototype():
    total = TAPS * NFFT
    offsets = np.arange(total, dtype=np.float64)
    shifted = (offsets - 0.5 * total + 0.5) / NFFT
    window = 0.5 - 0.5 * np.cos(2.0 * math.pi / total * (offsets + 0.5))
    return (np.sinc(shifted) * window).reshape(TAPS, NFFT).astype(np.float32)


def turns(u):
    whole = jnp.floor(u + 0.5)
    theta = (u - whole) * (0.5 * math.pi)
    sq = theta * theta
    sin = theta * (1.0 + sq * (-1.0 / 6 + sq * (1.0 / 120 + sq * (-1.0 / 5040 + sq * (1.0 / 362880)))))
    cos = 1.0 + sq * (-0.5 + sq * (1.0 / 24 + sq * (-1.0 / 720 + sq * (1.0 / 40320))))
    quad = whole.astype(i32)
    odd = (quad & 1) != 0
    cos_out = jnp.where(odd, sin, cos)
    sin_out = jnp.where(odd, cos, sin)
    cos_out = jnp.where(((quad + 1) & 2) != 0, -cos_out, cos_out)
    sin_out = jnp.where((quad & 2) != 0, -sin_out, sin_out)
    return cos_out, sin_out


def column(row):
    return jnp.broadcast_to(row, (128, 128)).T


def lane_iota(rows=128, cols=128):
    return lax.broadcasted_iota(i32, (rows, cols), 1)


def main_kernel(
    v_hbm, taps_hbm, bins_hbm, bins_smem, map_hbm, beam_hbm, delays_hbm,
    series_hbm, beams_hbm,
    vbuf, taps_ref, bins_row, map_row, beam_row, taps_b, table, filtered, spread, stage, recv, delays, weights, select, beam_sel,
    half, turned, xt, series, stage2,
    v_sem, small_sem, d_sem, send_sem, recv_sem, send2_sem, recv2_sem, out_sem,
):
    me_tm, me_f = lax.axis_index("tm"), lax.axis_index("freq")
    me = me_tm * FREQ + me_f
    barrier = pltpu.get_barrier_semaphore()

    def peer_id(i):
        peer = (me + i) & (NDEV - 1)
        return peer, (peer >> 5, peer & (FREQ - 1))

    def greet(i):
        pl.semaphore_signal(barrier, inc=1, device_id=peer_id(i)[1], device_id_type=MESH)

    def send(jc, i):
        peer, where = peer_id(i)
        pltpu.make_async_remote_copy(
            src_ref=stage.at[jc, peer], dst_ref=recv.at[jc, me], send_sem=send_sem.at[jc], recv_sem=recv_sem.at[jc],
            device_id=where, device_id_type=MESH,
        ).start()

    def ahead(act):
        @pl.loop(1, NDEV - 16 * EACH)
        def _(i):
            act(i)

    def beside(step, act):
        for u in range(EACH):
            act(NDEV - 16 * EACH + step * EACH + u)

    first = JB + TAPS - 1
    quarter = NFFT // 4

    def fetch_quarter(nq):
        @pl.loop(0, first)
        def _(f):
            at = pl.ds(pl.multiple_of(f * NFFT + nq * quarter, quarter), quarter)
            pltpu.make_async_copy(v_hbm.at[0, :, at], vbuf.at[:, at], v_sem.at[nq]).start()

    smalls = [
        pltpu.make_async_copy(src, dst, small_sem.at[n])
        for n, (src, dst) in enumerate(((taps_hbm, taps_ref), (bins_hbm, bins_row), (map_hbm, map_row), (beam_hbm, beam_row)))
    ]
    for small in smalls:
        small.start()
    fetch_quarter(0)
    smalls[0].wait()

    @pl.loop(0, NFFT // 256)
    def _(nb):
        at = pl.ds(pl.multiple_of(nb * 256, 256), 256)
        for k in range(TAPS):
            taps_b[k, :, at] = jnp.broadcast_to(taps_ref[k : k + 1, at], (8, 256)).astype(bf16)

    @pl.loop(1, 4)
    def _(nq):
        fetch_quarter(nq)

    for more in range(CHUNKS - 1):
        at = pl.ds((first + more * JB) * NFFT, JB * NFFT)
        pltpu.make_async_copy(v_hbm.at[0, :, at], vbuf.at[:, at], v_sem.at[4 + more]).start()
    delay_copy = pltpu.make_async_copy(delays_hbm, delays, d_sem)
    delay_copy.start()

    for small in smalls[1:]:
        small.wait()
    bins_col = column(bins_row[...].astype(f32)).astype(i32)
    low_cos, low_sin = turns(((bins_col * lane_iota()) & (NFFT - 1)).astype(f32) * (4.0 / NFFT))
    step_cos, step_sin = turns((bins_col & 31).astype(f32) * (4.0 / 32))
    scale = 1.0 / math.sqrt(NFFT)
    low_cos, low_neg = low_cos * scale, low_sin * -scale
    for cb in range(CHAN // 32):
        rows = slice(cb * 32, (cb + 1) * 32)
        real, imag, turn_real, turn_imag = low_cos[rows], low_neg[rows], step_cos[rows], -step_sin[rows]
        for h in range(NFFT // 128):
            at = slice(h * 128, (h + 1) * 128)
            table[rows, at] = real.astype(bf16)
            table[CHAN + cb * 32 : CHAN + (cb + 1) * 32, at] = imag.astype(bf16)
            real, imag = real * turn_real - imag * turn_imag, real * turn_imag + imag * turn_real

    def filter_block(jc, nb, rb):
        c0 = pl.multiple_of(nb * 256, 256)
        at = pl.ds(c0, 256)
        outer = {k: taps_b[k, :, at] for k in range(TAPS) if k not in CENTRAL}
        central = {k: jnp.broadcast_to(taps_ref[k : k + 1, at], (8, 256)) for k in CENTRAL}
        small = [None] * JB
        large = [None] * JB
        for i in range(JB + TAPS - 1):
            x = vbuf[rb * 8 : (rb + 1) * 8, pl.ds(pl.multiple_of((jc * JB + i) * NFFT + c0, 256), 256)]
            wide = None
            for j in range(max(0, i - TAPS + 1), min(JB - 1, i) + 1):
                k = i - j
                if k in CENTRAL:
                    wide = x.astype(f32) if wide is None else wide
                    term = central[k] * wide
                    large[j] = term if large[j] is None else large[j] + term
                else:
                    term = outer[k] * x
                    small[j] = term if small[j] is None else small[j] + term
            j = i - TAPS + 1
            if j >= 0:
                filtered[rb * 128 + j * 8 : rb * 128 + (j + 1) * 8, at] = (large[j] + small[j].astype(f32)).astype(bf16)

    def channelize(jc, act):
        if jc > 0:
            at = pl.ds(0, JB * NFFT)
            pltpu.make_async_copy(v_hbm.at[0, :, at], vbuf.at[:, at], v_sem.at[3 + jc]).wait()
        ahead(act)
        @pl.loop(0, NFFT // 256)
        def _(nb):
            if jc == 0:
                @pl.when(lax.rem(nb, 4) == 0)
                def _():
                    at = pl.ds(0, first * quarter)
                    pltpu.make_async_copy(v_hbm.at[0, :, at], vbuf.at[:, at], v_sem.at[nb // 4]).wait()

            beside(nb, act)
            for rb in range(SIGD // 8):
                filter_block(jc, nb, rb)

        for nt in range(2):
            out = lax.dot_general(
                table[...], filtered[nt * 256 : (nt + 1) * 256, :], (((1,), (1,)), ((), ())), preferred_element_type=f32
            )
            for r in range(2):
                for part in range(2):
                    rb = nt * 2 + part
                    spread[pl.ds(rb * 2 + r, CHAN, stride=8), :] = out[r * CHAN : (r + 1) * CHAN, part * 128 : (part + 1) * 128]

        @pl.loop(0, CHAN // 16)
        def _(cb):
            for i in range(16):
                c = cb * 16 + i
                stage[jc, c] = spread[pl.ds(pl.multiple_of(c * 8, 8), 8), :].astype(bf16)

        if jc == 0:
            pl.semaphore_wait(barrier, NDEV - 1)
        pltpu.make_async_copy(stage.at[jc, me], recv.at[jc, me], recv_sem.at[jc]).start()

    channelize(0, greet)
    channelize(1, functools.partial(send, 0))
    channelize(2, functools.partial(send, 1))

    delay_copy.wait()
    bin_value = bins_smem[me].astype(f32) * (4.0 / NFFT)

    ahead(functools.partial(send, 2))

    @pl.loop(0, BEAMS // 32)
    def _(pb):
        beside(pb, functools.partial(send, 2))
        row = pl.multiple_of(pb * 32, 32)
        for part in range(4):
            cos, sin = turns(delays[pl.ds(row, 32), part * 256 : (part + 1) * 256] * bin_value)
            weights[pl.ds(row, 32), part * 256 : (part + 1) * 256] = cos.astype(bf16)
            weights[pl.ds(BEAMS + row, 32), part * 256 : (part + 1) * 256] = sin.astype(bf16)

    lanes = lane_iota()
    signal = (lanes // 4) * SIGD + lax.rem(lanes, 4) * 8
    for ab in range(ANT // 128):
        wanted = column(map_row[:, ab * 128 : (ab + 1) * 128].astype(f32)).astype(i32)
        for s8 in range(8):
            select[ab * 128 : (ab + 1) * 128, s8 * 128 : (s8 + 1) * 128] = jnp.where(wanted == signal + s8, 1.0, 0.0).astype(bf16)
    for bb in range(BEAMS // 128):
        wanted = column(beam_row[:, bb * 128 : (bb + 1) * 128].astype(f32)).astype(i32)
        for pb in range(BEAMS // 128):
            beam_sel[bb * 128 : (bb + 1) * 128, pb * 128 : (pb + 1) * 128] = jnp.where(wanted == lanes + pb * 128, 1.0, 0.0).astype(bf16)
    def beamform(low, high):
        for jc in range(low, high):
            pltpu.make_async_copy(stage.at[jc], recv.at[jc], recv_sem.at[jc]).wait()

            @pl.loop(0, TM)
            def _(q):
                for f in range(FREQ):
                    half[f * 8 : (f + 1) * 8, :] = recv[jc, q * FREQ + f].astype(f32)
                for r in range(2):
                    turned[...] = half[pl.ds(r, 128, stride=2), :].T
                    row = pl.multiple_of((jc - low) * 128 + (r * TM + q) * JB, JB)
                    for s8 in range(8):
                        xt[pl.ds(row, JB), s8 * 128 : (s8 + 1) * 128] = turned[pl.ds(s8, JB, stride=8), :].astype(bf16)

        count = high - low
        cols = slice(low * 128, high * 128)

        @pl.loop(0, ANT // 256)
        def _(ab):
            rows = pl.ds(pl.multiple_of(ab * 256, 256), 256)
            series[rows, cols] = lax.dot_general(
                select[rows, :], xt[0 : count * 128, :], (((1,), (1,)), ((), ())), preferred_element_type=f32
            ).astype(bf16)

        pltpu.make_async_copy(series.at[:, cols], series_hbm.at[:, cols], out_sem.at[low]).start()
        ordered = series[:, cols]
        sign = jnp.where(lane_iota(BEAMS // 2, 128) < 64, 1.0 / math.sqrt(ANT), -1.0 / math.sqrt(ANT))
        formed = []
        for pb in range(2):
            cos_part = jnp.dot(weights[pb * 256 : (pb + 1) * 256, :], ordered, preferred_element_type=f32)
            sin_part = jnp.dot(weights[BEAMS + pb * 256 : BEAMS + (pb + 1) * 256, :], ordered, preferred_element_type=f32)
            turn = [sign * pltpu.roll(sin_part[:, n * 128 : (n + 1) * 128], 64, 1) for n in range(count)]
            formed.append((cos_part * (1.0 / math.sqrt(ANT)) + jnp.concatenate(turn, 1)).astype(bf16))
        picked = jnp.dot(beam_sel[...], jnp.concatenate(formed, 0), preferred_element_type=f32)
        for jc in range(low, high):
            part = picked[:, (jc - low) * 128 : (jc - low + 1) * 128]
            stage2[jc] = part.astype(bf16).reshape(FREQ, 16, 128)
            pltpu.make_async_copy(stage2.at[jc, me_f], beams_hbm.at[jc, me_f], recv2_sem.at[jc]).start()

            @pl.loop(1, FREQ)
            def _(i):
                peer = (me_f + i) & (FREQ - 1)
                pltpu.make_async_remote_copy(
                    src_ref=stage2.at[jc, peer], dst_ref=beams_hbm.at[jc, me_f], send_sem=send2_sem.at[jc],
                    recv_sem=recv2_sem.at[jc], device_id=(me_tm, peer), device_id_type=MESH,
                ).start()

    beamform(0, 2)
    beamform(2, 3)

    for jc in range(CHUNKS):
        sent = stage.at[jc, pl.ds(0, NDEV - 1)]
        pltpu.make_async_copy(sent, sent, send_sem.at[jc]).wait()
        sent = stage2.at[jc, pl.ds(0, FREQ - 1)]
        pltpu.make_async_copy(sent, sent, send2_sem.at[jc]).wait()
    for low, high in ((0, 2), (2, 3)):
        cols = slice(low * 128, high * 128)
        pltpu.make_async_copy(series.at[:, cols], series_hbm.at[:, cols], out_sem.at[low]).wait()
    for jc in range(CHUNKS):
        pltpu.make_async_copy(stage2.at[jc], beams_hbm.at[jc], recv2_sem.at[jc]).wait()


def vis_kernel(series_ref, beams_hbm, vis_hbm, out_hbm, vis, beams_ref, ordered, sems, beam_sem, out_sem):
    fetch = pltpu.make_async_copy(beams_hbm, beams_ref, beam_sem)
    fetch.start()
    count = ANT // VSTEPS
    copies = []
    for step in range(VSTEPS):
        rows = slice(step * count, (step + 1) * count)
        part = series_ref[rows, :]
        swapped = []
        for jc in range(CHUNKS):
            chunk = part[:, jc * 128 : (jc + 1) * 128].astype(f32)
            sign = jnp.where(lane_iota(*chunk.shape) < 64, 1.0, -1.0)
            swapped.append((pltpu.roll(chunk, 64, 1) * sign).astype(bf16))
        pair = jnp.concatenate([part, jnp.concatenate(swapped, 1)], 0)
        for bb in range(4):
            cols = slice(bb * 256, (bb + 1) * 256)
            out = lax.dot_general(pair, series_ref[cols, :], (((1,), (1,)), ((), ())), preferred_element_type=f32)
            out = out * (1.0 / 192.0)
            vis[0, rows, cols] = out[:count]
            vis[1, rows, cols] = out[count:]
        copies.append(pltpu.make_async_copy(vis.at[:, rows, :], vis_hbm.at[0, :, rows, :], sems.at[step]))
        copies[-1].start()

    fetch.wait()
    moves = []
    for jc in range(CHUNKS):
        row = lax.broadcasted_iota(i32, (128, 512), 0)
        to = (row >> 6) * 256 + ((row >> 4) & 3) * 48 + jc * JB + (row & 15)
        moves.append(jnp.where(to == lane_iota(128, 512), 1.0, 0.0).astype(bf16))
    moves = jnp.concatenate(moves, 0)
    for cb in range(FREQ // 8):
        found = jnp.concatenate([beams_ref[jc, cb * 128 : (cb + 1) * 128, :] for jc in range(CHUNKS)], 1)
        total = jnp.dot(found, moves, preferred_element_type=f32)
        for u in range(8):
            for r in range(2):
                rows = slice(u * 16, (u + 1) * 16)
                ordered[:, cb * 8 + u, r, 0:128] = total[rows, r * 256 : r * 256 + 128]
                ordered[:, cb * 8 + u, r, 128:192] = total[rows, r * 256 + 128 : r * 256 + 192]
    copies.append(pltpu.make_async_copy(ordered, out_hbm, out_sem))
    copies[-1].start()
    for copy in copies:
        copy.wait()


def body(voltages, chan_bins, antenna_map, beam_index, delays):
    hbm = pl.BlockSpec(memory_space=pltpu.HBM)
    anywhere = pl.BlockSpec(memory_space=pl.ANY)
    dma = pltpu.SemaphoreType.DMA
    series, beams = pl.pallas_call(
        main_kernel,
        out_shape=(
            jax.ShapeDtypeStruct((ANT, 384), bf16),
            jax.ShapeDtypeStruct((CHUNKS, FREQ, 16, 128), bf16),
        ),
        in_specs=[hbm, hbm, hbm, pl.BlockSpec(memory_space=pltpu.SMEM), hbm, hbm, hbm],
        out_specs=(anywhere, anywhere),
        scratch_shapes=[
            pltpu.VMEM((SIGD, 63 * NFFT), bf16),
            pltpu.VMEM((TAPS, NFFT), f32),
            pltpu.VMEM((1, CHAN), i32),
            pltpu.VMEM((1, ANT), i32),
            pltpu.VMEM((1, BEAMS), i32),
            pltpu.VMEM((TAPS, 8, NFFT), bf16),
            pltpu.VMEM((2 * CHAN, NFFT), bf16),
            pltpu.VMEM((SIGD * JB, NFFT), bf16),
            pltpu.VMEM((CHAN * 8, 128), f32),
            pltpu.VMEM((CHUNKS, NDEV, 8, 128), bf16),
            pltpu.VMEM((CHUNKS, NDEV, 8, 128), bf16),
            pltpu.VMEM((BEAMS, ANT), f32),
            pltpu.VMEM((2 * BEAMS, ANT), bf16),
            pltpu.VMEM((ANT, ANT), bf16),
            pltpu.VMEM((BEAMS, BEAMS), bf16),
            pltpu.VMEM((256, 128), f32),
            pltpu.VMEM((128, 128), f32),
            pltpu.VMEM((256, ANT), bf16),
            pltpu.VMEM((ANT, 384), bf16),
            pltpu.VMEM((CHUNKS, FREQ, 16, 128), bf16),
            dma((6,)),
            dma((4,)),
            dma,
            dma((CHUNKS,)),
            dma((CHUNKS,)),
            dma((CHUNKS,)),
            dma((CHUNKS,)),
            dma((CHUNKS,)),
        ],
        compiler_params=pltpu.CompilerParams(
            collective_id=0, has_side_effects=True, vmem_limit_bytes=VMEM_LIMIT
        ),
        name="channelize",
    )(
        voltages,
        jnp.asarray(prototype()),
        chan_bins.reshape(1, CHAN),
        chan_bins,
        antenna_map.reshape(1, ANT),
        beam_index.reshape(1, BEAMS),
        delays,
    )
    visibilities, beam_volts = pl.pallas_call(
        vis_kernel,
        out_shape=(
            jax.ShapeDtypeStruct((1, 2, ANT, ANT), f32),
            jax.ShapeDtypeStruct((16, FREQ, 2, 192), f32),
        ),
        in_specs=[pl.BlockSpec(memory_space=pltpu.VMEM), hbm],
        out_specs=(anywhere, anywhere),
        scratch_shapes=[
            pltpu.VMEM((2, ANT, ANT), f32),
            pltpu.VMEM((CHUNKS, FREQ * 16, 128), bf16),
            pltpu.VMEM((16, FREQ, 2, 192), f32),
            dma((VSTEPS,)),
            dma,
            dma,
        ],
        compiler_params=pltpu.CompilerParams(vmem_limit_bytes=VMEM_LIMIT),
        name="correlate",
    )(series, beams.reshape(CHUNKS, FREQ * 16, 128))
    return (visibilities, beam_volts)


def solution(mesh):
    return jax.shard_map(
        body,
        mesh=mesh,
        in_specs=(P("tm", "freq", None), P(), P(), P(), P()),
        out_specs=(P(("tm", "freq"), None, None, None), P("freq", "tm", None, None)),
        check_vma=False,
    )
```

```python
import functools
import math

import jax
import jax.numpy as jnp
import numpy as np
from jax import lax
from jax.experimental import pallas as pl
from jax.experimental.pallas import tpu as pltpu
from jax.sharding import PartitionSpec as P

NFFT = 4096
TAPS = 16
JB = 16
CHUNKS = 3
TM = 4
FREQ = 32
NDEV = TM * FREQ
SIGD = 32
CHAN = 128
BEAMS = 512
ANT = 1024
CENTRAL = (7, 8)
EACH = 7
VSTEPS = 4
VMEM_LIMIT = 60 * 1024 * 1024
FLAT = pl.DeviceIdType.LOGICAL
f32 = jnp.float32
bf16 = jnp.bfloat16
i32 = jnp.int32


def prototype():
    total = TAPS * NFFT
    offsets = np.arange(total, dtype=np.float64)
    shifted = (offsets - 0.5 * total + 0.5) / NFFT
    window = 0.5 - 0.5 * np.cos(2.0 * math.pi / total * (offsets + 0.5))
    return (np.sinc(shifted) * window).reshape(TAPS, NFFT).astype(np.float32)


def turns(u):
    whole = jnp.floor(u + 0.5)
    theta = (u - whole) * (0.5 * math.pi)
    sq = theta * theta
    sin = theta * (1.0 + sq * (-1.0 / 6 + sq * (1.0 / 120 + sq * (-1.0 / 5040 + sq * (1.0 / 362880)))))
    cos = 1.0 + sq * (-0.5 + sq * (1.0 / 24 + sq * (-1.0 / 720 + sq * (1.0 / 40320))))
    quad = whole.astype(i32)
    odd = (quad & 1) != 0
    cos_out = jnp.where(odd, sin, cos)
    sin_out = jnp.where(odd, cos, sin)
    cos_out = jnp.where(((quad + 1) & 2) != 0, -cos_out, cos_out)
    sin_out = jnp.where((quad & 2) != 0, -sin_out, sin_out)
    return cos_out, sin_out


def column(row):
    return jnp.broadcast_to(row, (128, 128)).T


def lane_iota(rows=128, cols=128):
    return lax.broadcasted_iota(i32, (rows, cols), 1)


def main_kernel(
    v_hbm, taps_hbm, bins_hbm, bins_smem, map_hbm, beam_hbm, delays_hbm,
    series_hbm, beams_hbm,
    vbuf, taps_ref, bins_row, map_row, beam_row, taps_b, table, filtered, spread, stage, recv, delays, weights, select, beam_sel,
    half, turned, xt, series, stage2,
    v_sem, small_sem, d_sem, send_sem, recv_sem, send2_sem, recv2_sem, out_sem,
):
    me_tm, me_f = lax.axis_index("tm"), lax.axis_index("freq")
    me = me_tm * FREQ + me_f
    barrier = pltpu.get_barrier_semaphore()

    def peer_id(i):
        peer = (me + i) & (NDEV - 1)
        return peer, peer

    def greet(i):
        pl.semaphore_signal(barrier, inc=1, device_id=peer_id(i)[1], device_id_type=FLAT)

    def send(jc, i):
        peer, where = peer_id(i)
        pltpu.make_async_remote_copy(
            src_ref=stage.at[jc, peer], dst_ref=recv.at[jc, me], send_sem=send_sem.at[jc], recv_sem=recv_sem.at[jc],
            device_id=where, device_id_type=FLAT,
        ).start()

    def ahead(act):
        @pl.loop(1, NDEV - 16 * EACH)
        def _(i):
            act(i)

    def beside(step, act, part):
        for u in range(part * EACH // 4, (part + 1) * EACH // 4):
            act(NDEV - 16 * EACH + step * EACH + u)

    first = JB + TAPS - 1
    quarter = NFFT // 4

    def fetch_quarter(nq):
        @pl.loop(0, first)
        def _(f):
            at = pl.ds(pl.multiple_of(f * NFFT + nq * quarter, quarter), quarter)
            pltpu.make_async_copy(v_hbm.at[0, :, at], vbuf.at[:, at], v_sem.at[nq]).start()

    smalls = [
        pltpu.make_async_copy(src, dst, small_sem.at[n])
        for n, (src, dst) in enumerate(((taps_hbm, taps_ref), (bins_hbm, bins_row), (map_hbm, map_row), (beam_hbm, beam_row)))
    ]
    for small in smalls:
        small.start()
    fetch_quarter(0)
    smalls[0].wait()

    @pl.loop(0, NFFT // 256)
    def _(nb):
        at = pl.ds(pl.multiple_of(nb * 256, 256), 256)
        for k in range(TAPS):
            taps_b[k, :, at] = jnp.broadcast_to(taps_ref[k : k + 1, at], (8, 256)).astype(bf16)

    @pl.loop(1, 4)
    def _(nq):
        fetch_quarter(nq)

    for more in range(CHUNKS - 1):
        at = pl.ds((first + more * JB) * NFFT, JB * NFFT)
        pltpu.make_async_copy(v_hbm.at[0, :, at], vbuf.at[:, at], v_sem.at[4 + more]).start()
    delay_copy = pltpu.make_async_copy(delays_hbm, delays, d_sem)
    delay_copy.start()

    for small in smalls[1:]:
        small.wait()
    bins_col = column(bins_row[...].astype(f32)).astype(i32)
    low_cos, low_sin = turns(((bins_col * lane_iota()) & (NFFT - 1)).astype(f32) * (4.0 / NFFT))
    step_cos, step_sin = turns((bins_col & 31).astype(f32) * (4.0 / 32))
    scale = 1.0 / math.sqrt(NFFT)
    low_cos, low_neg = low_cos * scale, low_sin * -scale
    for cb in range(CHAN // 32):
        rows = slice(cb * 32, (cb + 1) * 32)
        real, imag, turn_real, turn_imag = low_cos[rows], low_neg[rows], step_cos[rows], -step_sin[rows]
        for h in range(NFFT // 128):
            at = slice(h * 128, (h + 1) * 128)
            table[rows, at] = real.astype(bf16)
            table[CHAN + cb * 32 : CHAN + (cb + 1) * 32, at] = imag.astype(bf16)
            real, imag = real * turn_real - imag * turn_imag, real * turn_imag + imag * turn_real

    def filter_block(jc, nb, rb):
        c0 = pl.multiple_of(nb * 256, 256)
        at = pl.ds(c0, 256)
        outer = {k: taps_b[k, :, at] for k in range(TAPS) if k not in CENTRAL}
        central = {k: jnp.broadcast_to(taps_ref[k : k + 1, at], (8, 256)) for k in CENTRAL}
        small = [None] * JB
        large = [None] * JB
        for i in range(JB + TAPS - 1):
            x = vbuf[rb * 8 : (rb + 1) * 8, pl.ds(pl.multiple_of((jc * JB + i) * NFFT + c0, 256), 256)]
            wide = None
            for j in range(max(0, i - TAPS + 1), min(JB - 1, i) + 1):
                k = i - j
                if k in CENTRAL:
                    wide = x.astype(f32) if wide is None else wide
                    term = central[k] * wide
                    large[j] = term if large[j] is None else large[j] + term
                else:
                    term = outer[k] * x
                    small[j] = term if small[j] is None else small[j] + term
            j = i - TAPS + 1
            if j >= 0:
                filtered[rb * 128 + j * 8 : rb * 128 + (j + 1) * 8, at] = (large[j] + small[j].astype(f32)).astype(bf16)

    def channelize(jc, act):
        if jc > 0:
            at = pl.ds(0, JB * NFFT)
            pltpu.make_async_copy(v_hbm.at[0, :, at], vbuf.at[:, at], v_sem.at[3 + jc]).wait()
        ahead(act)
        @pl.loop(0, NFFT // 256)
        def _(nb):
            if jc == 0:
                @pl.when(lax.rem(nb, 4) == 0)
                def _():
                    at = pl.ds(0, first * quarter)
                    pltpu.make_async_copy(v_hbm.at[0, :, at], vbuf.at[:, at], v_sem.at[nb // 4]).wait()

            for rb in range(SIGD // 8):
                filter_block(jc, nb, rb)
            for part in range(4):
                beside(nb, act, part)

        for nt in range(2):
            out = lax.dot_general(
                table[...], filtered[nt * 256 : (nt + 1) * 256, :], (((1,), (1,)), ((), ())), preferred_element_type=f32
            )
            for r in range(2):
                for part in range(2):
                    rb = nt * 2 + part
                    spread[pl.ds(rb * 2 + r, CHAN, stride=8), :] = out[r * CHAN : (r + 1) * CHAN, part * 128 : (part + 1) * 128]

        @pl.loop(0, CHAN // 16)
        def _(cb):
            for i in range(16):
                c = cb * 16 + i
                stage[jc, c] = spread[pl.ds(pl.multiple_of(c * 8, 8), 8), :].astype(bf16)

        if jc == 0:
            pl.semaphore_wait(barrier, NDEV - 1)
        pltpu.make_async_copy(stage.at[jc, me], recv.at[jc, me], recv_sem.at[jc]).start()

    channelize(0, greet)
    channelize(1, functools.partial(send, 0))
    channelize(2, functools.partial(send, 1))

    delay_copy.wait()
    bin_value = bins_smem[me].astype(f32) * (4.0 / NFFT)

    ahead(functools.partial(send, 2))

    @pl.loop(0, BEAMS // 32)
    def _(pb):
        row = pl.multiple_of(pb * 32, 32)
        for part in range(4):
            cos, sin = turns(delays[pl.ds(row, 32), part * 256 : (part + 1) * 256] * bin_value)
            weights[pl.ds(row, 32), part * 256 : (part + 1) * 256] = cos.astype(bf16)
            weights[pl.ds(BEAMS + row, 32), part * 256 : (part + 1) * 256] = sin.astype(bf16)
            beside(pb, functools.partial(send, 2), part)

    lanes = lane_iota()
    signal = (lanes // 4) * SIGD + lax.rem(lanes, 4) * 8
    for ab in range(ANT // 128):
        wanted = column(map_row[:, ab * 128 : (ab + 1) * 128].astype(f32)).astype(i32)
        for s8 in range(8):
            select[ab * 128 : (ab + 1) * 128, s8 * 128 : (s8 + 1) * 128] = jnp.where(wanted == signal + s8, 1.0, 0.0).astype(bf16)
    for bb in range(BEAMS // 128):
        wanted = column(beam_row[:, bb * 128 : (bb + 1) * 128].astype(f32)).astype(i32)
        for pb in range(BEAMS // 128):
            beam_sel[bb * 128 : (bb + 1) * 128, pb * 128 : (pb + 1) * 128] = jnp.where(wanted == lanes + pb * 128, 1.0, 0.0).astype(bf16)
    def beamform(low, high):
        for jc in range(low, high):
            pltpu.make_async_copy(stage.at[jc], recv.at[jc], recv_sem.at[jc]).wait()

            @pl.loop(0, TM)
            def _(q):
                for f in range(FREQ):
                    half[f * 8 : (f + 1) * 8, :] = recv[jc, q * FREQ + f].astype(f32)
                for r in range(2):
                    turned[...] = half[pl.ds(r, 128, stride=2), :].T
                    row = pl.multiple_of((jc - low) * 128 + (r * TM + q) * JB, JB)
                    for s8 in range(8):
                        xt[pl.ds(row, JB), s8 * 128 : (s8 + 1) * 128] = turned[pl.ds(s8, JB, stride=8), :].astype(bf16)

        count = high - low
        cols = slice(low * 128, high * 128)

        @pl.loop(0, ANT // 256)
        def _(ab):
            rows = pl.ds(pl.multiple_of(ab * 256, 256), 256)
            series[rows, cols] = lax.dot_general(
                select[rows, :], xt[0 : count * 128, :], (((1,), (1,)), ((), ())), preferred_element_type=f32
            ).astype(bf16)

        pltpu.make_async_copy(series.at[:, cols], series_hbm.at[:, cols], out_sem.at[low]).start()
        ordered = series[:, cols]
        sign = jnp.where(lane_iota(BEAMS // 2, 128) < 64, 1.0 / math.sqrt(ANT), -1.0 / math.sqrt(ANT))
        formed = []
        for pb in range(2):
            cos_part = jnp.dot(weights[pb * 256 : (pb + 1) * 256, :], ordered, preferred_element_type=f32)
            sin_part = jnp.dot(weights[BEAMS + pb * 256 : BEAMS + (pb + 1) * 256, :], ordered, preferred_element_type=f32)
            turn = [sign * pltpu.roll(sin_part[:, n * 128 : (n + 1) * 128], 64, 1) for n in range(count)]
            formed.append((cos_part * (1.0 / math.sqrt(ANT)) + jnp.concatenate(turn, 1)).astype(bf16))
        picked = jnp.dot(beam_sel[...], jnp.concatenate(formed, 0), preferred_element_type=f32)
        for jc in range(low, high):
            part = picked[:, (jc - low) * 128 : (jc - low + 1) * 128]
            stage2[jc] = part.astype(bf16).reshape(FREQ, 16, 128)
            pltpu.make_async_copy(stage2.at[jc, me_f], beams_hbm.at[jc, me_f], recv2_sem.at[jc]).start()

            @pl.loop(1, FREQ)
            def _(i):
                peer = (me_f + i) & (FREQ - 1)
                pltpu.make_async_remote_copy(
                    src_ref=stage2.at[jc, peer], dst_ref=beams_hbm.at[jc, me_f], send_sem=send2_sem.at[jc],
                    recv_sem=recv2_sem.at[jc], device_id=me_tm * FREQ + peer, device_id_type=FLAT,
                ).start()

    beamform(0, 2)
    beamform(2, 3)

    for jc in range(CHUNKS):
        sent = stage.at[jc, pl.ds(0, NDEV - 1)]
        pltpu.make_async_copy(sent, sent, send_sem.at[jc]).wait()
        sent = stage2.at[jc, pl.ds(0, FREQ - 1)]
        pltpu.make_async_copy(sent, sent, send2_sem.at[jc]).wait()
    for low, high in ((0, 2), (2, 3)):
        cols = slice(low * 128, high * 128)
        pltpu.make_async_copy(series.at[:, cols], series_hbm.at[:, cols], out_sem.at[low]).wait()
    for jc in range(CHUNKS):
        pltpu.make_async_copy(stage2.at[jc], beams_hbm.at[jc], recv2_sem.at[jc]).wait()


def vis_kernel(series_ref, beams_hbm, vis_hbm, out_hbm, vis, beams_ref, ordered, sems, beam_sem, out_sem):
    fetch = pltpu.make_async_copy(beams_hbm, beams_ref, beam_sem)
    fetch.start()
    count = ANT // VSTEPS
    copies = []
    for step in range(VSTEPS):
        rows = slice(step * count, (step + 1) * count)
        part = series_ref[rows, :]
        swapped = []
        for jc in range(CHUNKS):
            chunk = part[:, jc * 128 : (jc + 1) * 128].astype(f32)
            sign = jnp.where(lane_iota(*chunk.shape) < 64, 1.0, -1.0)
            swapped.append((pltpu.roll(chunk, 64, 1) * sign).astype(bf16))
        pair = jnp.concatenate([part, jnp.concatenate(swapped, 1)], 0)
        for bb in range(4):
            cols = slice(bb * 256, (bb + 1) * 256)
            out = lax.dot_general(pair, series_ref[cols, :], (((1,), (1,)), ((), ())), preferred_element_type=f32)
            out = out * (1.0 / 192.0)
            vis[0, rows, cols] = out[:count]
            vis[1, rows, cols] = out[count:]
        copies.append(pltpu.make_async_copy(vis.at[:, rows, :], vis_hbm.at[0, :, rows, :], sems.at[step]))
        copies[-1].start()

    fetch.wait()
    moves = []
    for jc in range(CHUNKS):
        row = lax.broadcasted_iota(i32, (128, 512), 0)
        to = (row >> 6) * 256 + ((row >> 4) & 3) * 48 + jc * JB + (row & 15)
        moves.append(jnp.where(to == lane_iota(128, 512), 1.0, 0.0).astype(bf16))
    moves = jnp.concatenate(moves, 0)
    for cb in range(FREQ // 8):
        found = jnp.concatenate([beams_ref[jc, cb * 128 : (cb + 1) * 128, :] for jc in range(CHUNKS)], 1)
        total = jnp.dot(found, moves, preferred_element_type=f32)
        for u in range(8):
            for r in range(2):
                rows = slice(u * 16, (u + 1) * 16)
                ordered[:, cb * 8 + u, r, 0:128] = total[rows, r * 256 : r * 256 + 128]
                ordered[:, cb * 8 + u, r, 128:192] = total[rows, r * 256 + 128 : r * 256 + 192]
    copies.append(pltpu.make_async_copy(ordered, out_hbm, out_sem))
    copies[-1].start()
    for copy in copies:
        copy.wait()


def body(voltages, chan_bins, antenna_map, beam_index, delays):
    hbm = pl.BlockSpec(memory_space=pltpu.HBM)
    anywhere = pl.BlockSpec(memory_space=pl.ANY)
    dma = pltpu.SemaphoreType.DMA
    series, beams = pl.pallas_call(
        main_kernel,
        out_shape=(
            jax.ShapeDtypeStruct((ANT, 384), bf16),
            jax.ShapeDtypeStruct((CHUNKS, FREQ, 16, 128), bf16),
        ),
        in_specs=[hbm, hbm, hbm, pl.BlockSpec(memory_space=pltpu.SMEM), hbm, hbm, hbm],
        out_specs=(anywhere, anywhere),
        scratch_shapes=[
            pltpu.VMEM((SIGD, 63 * NFFT), bf16),
            pltpu.VMEM((TAPS, NFFT), f32),
            pltpu.VMEM((1, CHAN), i32),
            pltpu.VMEM((1, ANT), i32),
            pltpu.VMEM((1, BEAMS), i32),
            pltpu.VMEM((TAPS, 8, NFFT), bf16),
            pltpu.VMEM((2 * CHAN, NFFT), bf16),
            pltpu.VMEM((SIGD * JB, NFFT), bf16),
            pltpu.VMEM((CHAN * 8, 128), f32),
            pltpu.VMEM((CHUNKS, NDEV, 8, 128), bf16),
            pltpu.VMEM((CHUNKS, NDEV, 8, 128), bf16),
            pltpu.VMEM((BEAMS, ANT), f32),
            pltpu.VMEM((2 * BEAMS, ANT), bf16),
            pltpu.VMEM((ANT, ANT), bf16),
            pltpu.VMEM((BEAMS, BEAMS), bf16),
            pltpu.VMEM((256, 128), f32),
            pltpu.VMEM((128, 128), f32),
            pltpu.VMEM((256, ANT), bf16),
            pltpu.VMEM((ANT, 384), bf16),
            pltpu.VMEM((CHUNKS, FREQ, 16, 128), bf16),
            dma((6,)),
            dma((4,)),
            dma,
            dma((CHUNKS,)),
            dma((CHUNKS,)),
            dma((CHUNKS,)),
            dma((CHUNKS,)),
            dma((CHUNKS,)),
        ],
        compiler_params=pltpu.CompilerParams(
            collective_id=0, has_side_effects=True, vmem_limit_bytes=VMEM_LIMIT
        ),
        name="channelize",
    )(
        voltages,
        jnp.asarray(prototype()),
        chan_bins.reshape(1, CHAN),
        chan_bins,
        antenna_map.reshape(1, ANT),
        beam_index.reshape(1, BEAMS),
        delays,
    )
    visibilities, beam_volts = pl.pallas_call(
        vis_kernel,
        out_shape=(
            jax.ShapeDtypeStruct((1, 2, ANT, ANT), f32),
            jax.ShapeDtypeStruct((16, FREQ, 2, 192), f32),
        ),
        in_specs=[pl.BlockSpec(memory_space=pltpu.VMEM), hbm],
        out_specs=(anywhere, anywhere),
        scratch_shapes=[
            pltpu.VMEM((2, ANT, ANT), f32),
            pltpu.VMEM((CHUNKS, FREQ * 16, 128), bf16),
            pltpu.VMEM((16, FREQ, 2, 192), f32),
            dma((VSTEPS,)),
            dma,
            dma,
        ],
        compiler_params=pltpu.CompilerParams(vmem_limit_bytes=VMEM_LIMIT),
        name="correlate",
    )(series, beams.reshape(CHUNKS, FREQ * 16, 128))
    return (visibilities, beam_volts)


def solution(mesh):
    return jax.shard_map(
        body,
        mesh=mesh,
        in_specs=(P("tm", "freq", None), P(), P(), P(), P()),
        out_specs=(P(("tm", "freq"), None, None, None), P("freq", "tm", None, None)),
        check_vma=False,
    )
```
